32 devices in a mesh: rep: 1, ctx: 32 (over z, y, x, core), fsdp: 1.
Axes of the slice: x: 2, y: 2, z: 4, core: 2. Of those that a mesh axis runs over, the one named last changes fastest.
Arguments:
- projected_queries: bfloat16 [4096, 2, 2048], P(('rep', 'ctx'), None, 'fsdp'), may hold values from -5 to 5
- projected_keys: bfloat16 [4096, 2, 256], P(('rep', 'ctx'), None, 'fsdp'), may hold values from -5 to 5
- projected_values: bfloat16 [4096, 2, 256], P(('rep', 'ctx'), None, 'fsdp'), may hold values from -6 to 6
- output_gradient: bfloat16 [4096, 2, 2048], P(('rep', 'ctx'), None, 'fsdp'), may hold values from -24 to 24
- normed_layer_input: bfloat16 [4096, 8192], P(('rep', 'ctx'), 'fsdp'), may hold values from -6 to 6
- segment: int32 [4096], P('rep'), may hold values from 0 to 2, as said below
- query_adapter_down: bfloat16 [16, 8192], P(None, 'fsdp'), may hold values from -0.0625 to 0.0625
- query_adapter_up: bfloat16 [16, 2, 2048], P(None, None, 'fsdp'), may hold values from -1.5 to 1.5
- value_adapter_down: bfloat16 [16, 8192], P(None, 'fsdp'), may hold values from -0.0625 to 0.0625
- value_adapter_up: bfloat16 [16, 2, 256], P(None, None, 'fsdp'), may hold values from -1.5 to 1.5
Outputs:
- grad_query: bfloat16 [4096, 2, 2048], P(('rep', 'ctx'), None, 'fsdp')
- grad_key: bfloat16 [4096, 2, 256], P(('rep', 'ctx'), None, 'fsdp')
- grad_value: bfloat16 [4096, 2, 256], P(('rep', 'ctx'), None, 'fsdp')
- query_down_gradient: float32 [16, 8192], P('rep', 'fsdp')
- query_up_gradient: float32 [16, 2, 2048], P('rep', None, 'fsdp')
- value_down_gradient: float32 [16, 8192], P('rep', 'fsdp')
- value_up_gradient: float32 [16, 2, 256], P('rep', None, 'fsdp')
The draws below stay inside these ranges and needn't reach their ends.
Inputs may be any that keep to these rules, and one draw needn't show every extreme that they name: `segment`: documents are packed cyclically: ids rise by one at each of two boundaries, and a third boundary returns to id 0, whose document continues at the start of the token order; all boundaries lie at least 1024 tokens from both ends.
All inputs are finite; a program needn't handle non-finite values.
Results may differ from the reference program's by a relative error of at most 0.0079.
Values may be sent and summed in bfloat16 or wider, within the bound.
A program may use at most 64 MiB of HBM per device.

```python
import jax
import jax.numpy as jnp
from jax import lax

MODEL_WIDTH = 8192
QUERY_HEADS = 32
KEY_VALUE_HEADS = 4
HEAD_SIZE = 128
ADAPTER_RANK = 16
GROUP = 1024
DOCUMENT_TOKENS = 4096


def unsigned_field(key, array_shape):
    return jnp.clip(jax.random.normal(key, array_shape, jnp.float32), -5.0, 5.0)


def draw_projected_keys(key, part):
    sign_field = unsigned_field(jax.random.fold_in(key, 11), (DOCUMENT_TOKENS, 2, KEY_VALUE_HEADS // 2 * HEAD_SIZE))
    return sign_field.astype(jnp.bfloat16)


def draw_projected_queries(key, part):
    sign_field = unsigned_field(jax.random.fold_in(key, 13), (DOCUMENT_TOKENS, 2, QUERY_HEADS // 2 * HEAD_SIZE))
    return sign_field.astype(jnp.bfloat16)


def draw_segment(key, part):
    span_count = DOCUMENT_TOKENS - 2 * GROUP + 1
    order = jax.random.permutation(jax.random.fold_in(key, 41), span_count)
    cuts = jnp.sort(order[:3].astype(jnp.int32)) + GROUP
    positions = jnp.arange(DOCUMENT_TOKENS, dtype=jnp.int32)
    passed = jnp.sum((positions[:, None] >= cuts[None, :]).astype(jnp.int32), axis=1)
    return jnp.where(passed == 3, 0, passed).astype(jnp.int32)


def levels(rng, extent, cuts, least, largest):
    def one(axis_at, parts):
        heights = jax.random.uniform(jax.random.fold_in(jax.random.fold_in(rng, 6), axis_at), (parts,), jnp.float32, least / len(cuts), largest / len(cuts))
        return jnp.repeat(jnp.exp(heights), extent[axis_at] // parts).reshape((-1,) + (1,) * (len(extent) - axis_at - 1))

    gain = one(*cuts[0])
    for cut in cuts[1:]:
        gain = gain * one(*cut)
    return gain


def centred(rng, extent, width, reach, cuts=(), kind=jnp.bfloat16):
    values = jax.random.normal(rng, extent, jnp.float32) * width
    if len(cuts) > 0:
        values = levels(rng, extent, cuts, -0.22, 0.18) * values
    return jnp.clip(values, min=-reach, max=reach).astype(kind)


def setup_inputs(seed: int = 0, part: int = 0) -> dict:
    seeds = jax.random.split(jax.random.key(seed), 11)
    part_keys = jax.random.split(jax.random.fold_in(seeds[10], part), 11)
    projected_queries = draw_projected_queries(jax.random.fold_in(jax.random.fold_in(seeds[10], part), 71), part)
    projected_keys = draw_projected_keys(jax.random.fold_in(jax.random.fold_in(seeds[10], part), 71), part)
    projected_values = centred(part_keys[2], (DOCUMENT_TOKENS, 2, KEY_VALUE_HEADS // 2 * HEAD_SIZE), 1.0, 6.0, ((0, 32),))
    output_gradient = centred(part_keys[3], (DOCUMENT_TOKENS, 2, QUERY_HEADS // 2 * HEAD_SIZE), 4.0, 24.0, ((0, 32),))
    normed_layer_input = centred(part_keys[4], (DOCUMENT_TOKENS, MODEL_WIDTH), 1.0, 6.0, ((0, 32),))
    segment = draw_segment(jax.random.fold_in(jax.random.fold_in(seeds[10], part), 71), part)
    query_adapter_down = centred(seeds[6], (ADAPTER_RANK, MODEL_WIDTH), MODEL_WIDTH ** -0.5, 0.0625)
    query_adapter_up = centred(seeds[7], (ADAPTER_RANK, 2, QUERY_HEADS // 2 * HEAD_SIZE), ADAPTER_RANK ** -0.5, 1.5)
    value_adapter_down = centred(seeds[8], (ADAPTER_RANK, MODEL_WIDTH), MODEL_WIDTH ** -0.5, 0.0625)
    value_adapter_up = centred(seeds[9], (ADAPTER_RANK, 2, KEY_VALUE_HEADS // 2 * HEAD_SIZE), ADAPTER_RANK ** -0.5, 1.5)
    return dict(projected_queries=projected_queries, projected_keys=projected_keys, projected_values=projected_values, output_gradient=output_gradient, normed_layer_input=normed_layer_input, segment=segment, query_adapter_down=query_adapter_down, query_adapter_up=query_adapter_up, value_adapter_down=value_adapter_down, value_adapter_up=value_adapter_up)


adapter_scale = 2.0


def group_backward(items):
    query_part, grad_part, key_rows, value_rows, doc_ids = items
    scaling = HEAD_SIZE ** -0.5
    query_wide = query_part.astype(jnp.float32)
    grad_wide = grad_part.astype(jnp.float32)
    key_wide = key_rows.astype(jnp.float32)
    value_wide = value_rows.astype(jnp.float32)
    positions = jnp.arange(GROUP, dtype=jnp.int32)
    allowed = (positions[None, :] <= positions[:, None]) & (doc_ids[None, :] == doc_ids[:, None])
    scores = jnp.einsum("tgrd,lgd->tgrl", query_wide, key_wide) * scaling
    scores = jnp.where(allowed[:, None, None, :], scores, -jnp.inf)
    highest = jnp.max(scores, axis=-1, keepdims=True)
    weights = jnp.exp(scores - highest)
    weights = weights / jnp.sum(weights, axis=-1, keepdims=True)
    rounded = lax.optimization_barrier(weights.astype(jnp.bfloat16)).astype(jnp.float32)
    output = jnp.einsum("tgrl,lgd->tgrd", rounded, value_wide)
    row_dot = jnp.sum(grad_wide * output, axis=-1, keepdims=True)
    grad_weights = jnp.einsum("tgrd,lgd->tgrl", grad_wide, value_wide)
    grad_scores = lax.optimization_barrier((weights * (grad_weights - row_dot)).astype(jnp.bfloat16)).astype(jnp.float32)
    query_grad = jnp.einsum("tgrl,lgd->tgrd", grad_scores, key_wide) * scaling
    key_grad = jnp.einsum("tgrl,tgrd->lgd", grad_scores, query_wide) * scaling
    value_grad = jnp.einsum("tgrl,tgrd->lgd", rounded, grad_wide)
    return query_grad, key_grad, value_grad


def reference(projected_queries, projected_keys, projected_values, output_gradient, normed_layer_input, segment, query_adapter_down, query_adapter_up, value_adapter_down, value_adapter_up):
    key_value_heads = KEY_VALUE_HEADS // 2
    head_repeat = QUERY_HEADS // KEY_VALUE_HEADS
    groups = DOCUMENT_TOKENS // GROUP
    query_grads = []
    key_grads = []
    value_grads = []
    for half_index in range(2):
        offset = half_index * (GROUP // 2)
        query_part = jnp.roll(projected_queries[:, half_index], -offset, axis=0).reshape(groups, GROUP, key_value_heads, head_repeat, HEAD_SIZE)
        grad_part = jnp.roll(output_gradient[:, half_index], -offset, axis=0).reshape(groups, GROUP, key_value_heads, head_repeat, HEAD_SIZE)
        key_rows = jnp.roll(projected_keys[:, half_index], -offset, axis=0).reshape(groups, GROUP, key_value_heads, HEAD_SIZE)
        value_rows = jnp.roll(projected_values[:, half_index], -offset, axis=0).reshape(groups, GROUP, key_value_heads, HEAD_SIZE)
        doc_ids = jnp.roll(segment, -offset).reshape(groups, GROUP)
        query_grad, key_grad, value_grad = lax.map(group_backward, (query_part, grad_part, key_rows, value_rows, doc_ids))
        query_grads.append(jnp.roll(query_grad.reshape(DOCUMENT_TOKENS, -1), offset, axis=0))
        key_grads.append(jnp.roll(key_grad.reshape(DOCUMENT_TOKENS, -1), offset, axis=0))
        value_grads.append(jnp.roll(value_grad.reshape(DOCUMENT_TOKENS, -1), offset, axis=0))
    grad_query = jnp.stack(query_grads, axis=1).astype(jnp.bfloat16)
    grad_key = jnp.stack(key_grads, axis=1).astype(jnp.bfloat16)
    grad_value = jnp.stack(value_grads, axis=1).astype(jnp.bfloat16)
    query_flattened_rows = grad_query.reshape(DOCUMENT_TOKENS, -1)
    value_flattened_rows = grad_value.reshape(DOCUMENT_TOKENS, -1)
    query_down_part = jnp.dot(normed_layer_input, query_adapter_down.T, preferred_element_type=jnp.float32).astype(jnp.bfloat16)
    value_down_part = jnp.dot(normed_layer_input, value_adapter_down.T, preferred_element_type=jnp.float32).astype(jnp.bfloat16)
    query_up_part = jnp.dot(query_flattened_rows, query_adapter_up.reshape(ADAPTER_RANK, -1).T, preferred_element_type=jnp.float32).astype(jnp.bfloat16)
    value_up_part = jnp.dot(value_flattened_rows, value_adapter_up.reshape(ADAPTER_RANK, -1).T, preferred_element_type=jnp.float32).astype(jnp.bfloat16)
    query_up_gradient = adapter_scale * jnp.dot(query_down_part.T, query_flattened_rows, preferred_element_type=jnp.float32).reshape(ADAPTER_RANK, 2, -1)
    value_up_gradient = adapter_scale * jnp.dot(value_down_part.T, value_flattened_rows, preferred_element_type=jnp.float32).reshape(ADAPTER_RANK, 2, -1)
    query_down_gradient = adapter_scale * jnp.dot(query_up_part.T, normed_layer_input, preferred_element_type=jnp.float32)
    value_down_gradient = adapter_scale * jnp.dot(value_up_part.T, normed_layer_input, preferred_element_type=jnp.float32)
    return (grad_query, grad_key, grad_value, query_down_gradient, query_up_gradient, value_down_gradient, value_up_gradient)
```

```python
import functools
import math

import jax
import jax.numpy as jnp
from jax import lax
from jax.experimental import pallas as pl
from jax.experimental.pallas import tpu as pltpu
from jax.sharding import PartitionSpec as P

MESH = pl.DeviceIdType.MESH
MASKED = -1e30

QUERY_HEADS = 32
KEY_VALUE_HEADS = 4
HEAD_SIZE = 128
GROUP = 1024


adapter_scale = 2.0


def attention_kernel(
    ctx,
    devs,
    q_ref,
    do_ref,
    kv_ref,
    seg_ref,
    dq_ref,
    gkv_ref,
    kv_buf,
    part_send,
    part_recv,
    own_part,
    p_scr,
    ds_scr,
    bias,
    g_send,
    g_recv,
    r_send,
    r_recv,
):
    kv_heads = kv_ref.shape[1]
    tok = kv_ref.shape[2]
    repeat = q_ref.shape[1] // kv_heads
    mid = devs // 2
    scaling = HEAD_SIZE ** (-0.5)
    exponent = scaling * math.log2(math.e)
    me = lax.axis_index("ctx")
    p0 = lax.rem(me, devs)
    small = p0 // mid
    big = 1 - small
    ps = lax.rem(p0, mid)

    def ahead(d):
        return lax.rem(me + d, ctx)

    def behind(d):
        return lax.rem(me + ctx - d, ctx)

    barrier = pltpu.get_barrier_semaphore()
    for d in range(1, devs):
        pl.semaphore_signal(barrier, inc=1, device_id={"ctx": ahead(d)}, device_id_type=MESH)
        pl.semaphore_signal(barrier, inc=1, device_id={"ctx": behind(d)}, device_id_type=MESH)
    pl.semaphore_wait(barrier, 2 * (devs - 1))

    def gather_copy(h, d):
        return pltpu.make_async_remote_copy(
            src_ref=kv_ref.at[h],
            dst_ref=kv_buf.at[h, d],
            send_sem=g_send.at[h, d],
            recv_sem=g_recv.at[h, d],
            device_id={"ctx": ahead(d)},
            device_id_type=MESH,
        )

    def return_copy(h, g, d):
        return pltpu.make_async_remote_copy(
            src_ref=part_send.at[h, g, d],
            dst_ref=part_recv.at[h, g, d],
            send_sem=r_send.at[h, g, d],
            recv_sem=r_recv.at[h, g, d],
            device_id={"ctx": behind(d)},
            device_id_type=MESH,
        )

    for d in range(1, mid):

        @pl.when(ps + d < mid)
        def _():
            gather_copy(small, d).start()

    for d in range(1, devs):

        @pl.when((ps + d >= mid) & (ps + d < devs))
        def _():
            gather_copy(small, d).start()

    for d in range(1, mid):

        @pl.when(ps + d < mid)
        def _():
            gather_copy(big, d).start()

    for h in range(2):
        kv_buf[h, 0] = kv_ref[h]
    for d in range(1, mid):

        @pl.when(d > ps)
        def _():
            kv_buf[small, d] = jnp.zeros(kv_buf.shape[2:], kv_buf.dtype)

        @pl.when(d > ps)
        def _():
            kv_buf[big, mid + d] = jnp.zeros(kv_buf.shape[2:], kv_buf.dtype)

    own_ids = jnp.transpose(
        jnp.broadcast_to(seg_ref[pl.ds(me, 1), :].astype(jnp.float32), (tok, tok))
    )
    rows = lax.broadcasted_iota(jnp.int32, (tok, tok), 0)
    columns = lax.broadcasted_iota(jnp.int32, (tok, tok), 1)
    for d in range(devs):
        ids = seg_ref[pl.ds(behind(d), 1), :].astype(jnp.float32)
        block = jnp.where(own_ids == ids, 0.0, MASKED)
        if d == 0:
            block = jnp.where(columns <= rows, block, MASKED)
        bias[:, d * tok : (d + 1) * tok] = block

    def attend(h, slots, limit):
        keys = slots * tok

        def head_group(g, carry):
            k = kv_buf[h, :slots, g, :, :HEAD_SIZE].reshape(keys, HEAD_SIZE)
            v = kv_buf[h, :slots, g, :, HEAD_SIZE:].reshape(keys, HEAD_SIZE)

            def one_head(r, inner):
                q = q_ref[h, g * repeat + r]
                do = do_ref[h, g * repeat + r]
                s = lax.dot_general(
                    q, k, (((1,), (1,)), ((), ())), preferred_element_type=jnp.float32
                )
                dp = lax.dot_general(
                    do, v, (((1,), (1,)), ((), ())), preferred_element_type=jnp.float32
                )
                at = lax.broadcasted_iota(jnp.int32, (1, keys), 1)
                reach = jnp.where(at < limit * tok, 0.0, MASKED)
                t = s * exponent + (bias[:, :keys] + reach)
                e = jnp.exp2(t - jnp.max(t, axis=1, keepdims=True))
                w = e * (1.0 / jnp.sum(e, axis=1, keepdims=True))
                low = w.astype(jnp.bfloat16)
                dot = jnp.sum(low.astype(jnp.float32) * dp, axis=1, keepdims=True)
                ds = (w * (dp - dot)).astype(jnp.bfloat16)
                at_row = pl.multiple_of(r * tok, tok)
                p_scr[pl.ds(at_row, tok), :keys] = low
                ds_scr[pl.ds(at_row, tok), :keys] = ds
                dq = jnp.dot(ds, k, preferred_element_type=jnp.float32) * scaling
                dq_ref[h, g * repeat + r] = dq.astype(jnp.bfloat16)
                return inner

            lax.fori_loop(0, repeat, one_head, 0, unroll=2)
            q_all = q_ref[h, pl.ds(g * repeat, repeat)].reshape(repeat * tok, HEAD_SIZE)
            do_all = do_ref[h, pl.ds(g * repeat, repeat)].reshape(repeat * tok, HEAD_SIZE)
            dk = lax.dot_general(
                q_all,
                ds_scr[:, :keys],
                (((0,), (0,)), ((), ())),
                preferred_element_type=jnp.float32,
            )
            dv = lax.dot_general(
                do_all,
                p_scr[:, :keys],
                (((0,), (0,)), ((), ())),
                preferred_element_type=jnp.float32,
            )
            for d in range(slots):
                dk_block = jnp.transpose(dk[:, d * tok : (d + 1) * tok]) * scaling
                dv_block = jnp.transpose(dv[:, d * tok : (d + 1) * tok])
                if d == 0:
                    own_part[h, g, :, :HEAD_SIZE] = dk_block
                    own_part[h, g, :, HEAD_SIZE:] = dv_block
                else:
                    part_send[h, g, d, :, :HEAD_SIZE] = dk_block.astype(jnp.bfloat16)
                    part_send[h, g, d, :, HEAD_SIZE:] = dv_block.astype(jnp.bfloat16)
            for d in range(1, slots):

                @pl.when(d < limit)
                def _():
                    return_copy(h, g, d).start()

            return carry

        lax.fori_loop(0, kv_heads, head_group, 0)

    for d in range(1, mid):

        @pl.when(d <= ps)
        def _():
            gather_copy(small, d).wait_recv()

    attend(small, mid, ps + 1)

    for d in range(1, devs):

        @pl.when(d <= ps + mid)
        def _():
            gather_copy(big, d).wait_recv()

    attend(big, devs, ps + mid + 1)

    for d in range(1, devs):
        for g in range(kv_heads):

            @pl.when(ps + d < devs)
            def _():
                return_copy(small, g, d).wait_recv()
                own_part[small, g] = own_part[small, g] + part_recv[small, g, d].astype(
                    jnp.float32
                )

    for d in range(1, mid):
        for g in range(kv_heads):

            @pl.when(ps + d < mid)
            def _():
                return_copy(big, g, d).wait_recv()
                own_part[big, g] = own_part[big, g] + part_recv[big, g, d].astype(jnp.float32)

    gkv_ref[...] = own_part[...].astype(jnp.bfloat16)

    for d in range(1, devs):

        @pl.when(ps + d < devs)
        def _():
            gather_copy(small, d).wait_send()

        @pl.when(d <= ps + mid)
        def _():
            for g in range(kv_heads):
                return_copy(big, g, d).wait_send()

    for d in range(1, mid):

        @pl.when(ps + d < mid)
        def _():
            gather_copy(big, d).wait_send()

        @pl.when(d <= ps)
        def _():
            for g in range(kv_heads):
                return_copy(small, g, d).wait_send()


def attention_backward(q, do, kv, seg, devs):
    heads, tok = q.shape[1], q.shape[2]
    kv_heads = kv.shape[1]
    repeat = heads // kv_heads
    ctx = lax.axis_size("ctx")
    bf16, f32 = jnp.bfloat16, jnp.float32
    pair = 2 * HEAD_SIZE
    vmem = pl.BlockSpec(memory_space=pltpu.VMEM)
    return pl.pallas_call(
        functools.partial(attention_kernel, ctx, devs),
        out_shape=(
            jax.ShapeDtypeStruct(q.shape, bf16),
            jax.ShapeDtypeStruct(kv.shape, bf16),
        ),
        in_specs=[vmem] * 4,
        out_specs=(vmem, vmem),
        scratch_shapes=[
            pltpu.VMEM((2, devs, kv_heads, tok, pair), bf16),
            pltpu.VMEM((2, kv_heads, devs, tok, pair), bf16),
            pltpu.VMEM((2, kv_heads, devs, tok, pair), bf16),
            pltpu.VMEM((2, kv_heads, tok, pair), f32),
            pltpu.VMEM((repeat * tok, devs * tok), bf16),
            pltpu.VMEM((repeat * tok, devs * tok), bf16),
            pltpu.VMEM((tok, devs * tok), f32),
            pltpu.SemaphoreType.DMA((2, devs)),
            pltpu.SemaphoreType.DMA((2, devs)),
            pltpu.SemaphoreType.DMA((2, kv_heads, devs)),
            pltpu.SemaphoreType.DMA((2, kv_heads, devs)),
        ],
        compiler_params=pltpu.CompilerParams(
            collective_id=0, has_side_effects=True, vmem_limit_bytes=48 * 1024 * 1024
        ),
        name="attention_backward",
    )(q, do, kv, seg)


def on_device(
    projected_queries,
    projected_keys,
    projected_values,
    output_gradient,
    normed_layer_input,
    segment,
    query_adapter_down,
    query_adapter_up,
    value_adapter_down,
    value_adapter_up,
):
    tok_rows = projected_queries.shape[0]
    query_width = projected_queries.shape[2]
    key_width = projected_keys.shape[2]
    key_value_heads = key_width // HEAD_SIZE
    group_devs = GROUP // tok_rows
    query_heads = query_width // HEAD_SIZE

    def by_head(x, heads):
        return x.reshape(tok_rows, 2, heads, HEAD_SIZE).transpose(1, 2, 0, 3)

    keys_values = jnp.concatenate(
        [by_head(projected_keys, key_value_heads), by_head(projected_values, key_value_heads)],
        axis=3,
    )
    query_grad, pair_grad = attention_backward(
        by_head(projected_queries, query_heads),
        by_head(output_gradient, query_heads),
        keys_values,
        segment.reshape(-1, tok_rows),
        group_devs,
    )
    grad_query = query_grad.transpose(2, 0, 1, 3).reshape(tok_rows, 2, query_width)
    grad_key = pair_grad[..., :HEAD_SIZE].transpose(2, 0, 1, 3).reshape(tok_rows, 2, key_width)
    grad_value = pair_grad[..., HEAD_SIZE:].transpose(2, 0, 1, 3).reshape(tok_rows, 2, key_width)
    adapter_input = lax.psum(
        (
            jnp.dot(normed_layer_input, query_adapter_down.T, preferred_element_type=jnp.float32),
            jnp.dot(normed_layer_input, value_adapter_down.T, preferred_element_type=jnp.float32),
        ),
        "fsdp",
    )
    query_down_part = adapter_input[0].astype(jnp.bfloat16)
    value_down_part = adapter_input[1].astype(jnp.bfloat16)
    query_flattened_rows = grad_query.reshape(tok_rows, -1)
    value_flattened_rows = grad_value.reshape(tok_rows, -1)
    adapter_rank_rows = query_adapter_up.shape[0]
    adapter_output = lax.psum(
        (
            jnp.dot(
                query_flattened_rows,
                query_adapter_up.reshape(adapter_rank_rows, -1).T,
                preferred_element_type=jnp.float32,
            ),
            jnp.dot(
                value_flattened_rows,
                value_adapter_up.reshape(adapter_rank_rows, -1).T,
                preferred_element_type=jnp.float32,
            ),
        ),
        "fsdp",
    )
    query_up_part = adapter_output[0].astype(jnp.bfloat16)
    value_up_part = adapter_output[1].astype(jnp.bfloat16)
    local_down_query = jnp.dot(
        query_up_part.T, normed_layer_input, preferred_element_type=jnp.float32
    )
    local_up_query = jnp.dot(
        query_down_part.T, query_flattened_rows, preferred_element_type=jnp.float32
    ).reshape(adapter_rank_rows, 2, -1)
    local_down_value = jnp.dot(
        value_up_part.T, normed_layer_input, preferred_element_type=jnp.float32
    )
    local_up_value = jnp.dot(
        value_down_part.T, value_flattened_rows, preferred_element_type=jnp.float32
    ).reshape(adapter_rank_rows, 2, -1)
    gradient_totals = lax.psum(
        (local_down_query, local_up_query, local_down_value, local_up_value), "ctx"
    )
    return (
        grad_query,
        grad_key,
        grad_value,
        adapter_scale * gradient_totals[0],
        adapter_scale * gradient_totals[1],
        adapter_scale * gradient_totals[2],
        adapter_scale * gradient_totals[3],
    )


def solution(mesh):
    in_specs = (
        P(("rep", "ctx"), None, "fsdp"),
        P(("rep", "ctx"), None, "fsdp"),
        P(("rep", "ctx"), None, "fsdp"),
        P(("rep", "ctx"), None, "fsdp"),
        P(("rep", "ctx"), "fsdp"),
        P("rep"),
        P(None, "fsdp"),
        P(None, None, "fsdp"),
        P(None, "fsdp"),
        P(None, None, "fsdp"),
    )
    out_specs = (
        P(("rep", "ctx"), None, "fsdp"),
        P(("rep", "ctx"), None, "fsdp"),
        P(("rep", "ctx"), None, "fsdp"),
        P("rep", "fsdp"),
        P("rep", None, "fsdp"),
        P("rep", "fsdp"),
        P("rep", None, "fsdp"),
    )
    return jax.shard_map(
        on_device, mesh=mesh, in_specs=in_specs, out_specs=out_specs, check_vma=False
    )
```

```python
import functools
import math

import jax
import jax.numpy as jnp
from jax import lax
from jax.experimental import pallas as pl
from jax.experimental.pallas import tpu as pltpu
from jax.sharding import PartitionSpec as P

MESH = pl.DeviceIdType.MESH
MASKED = -1e30

QUERY_HEADS = 32
KEY_VALUE_HEADS = 4
HEAD_SIZE = 128
GROUP = 1024


adapter_scale = 2.0


def attention_kernel(
    ctx,
    devs,
    with_adapters,
    q_ref,
    do_ref,
    kv_ref,
    seg_ref,
    *refs,
):
    if with_adapters:
        x_ref, down_ref, q_up_ref, v_up_ref = refs[:4]
        dq_ref, gkv_ref, qd_out, qu_out, vd_out, vu_out = refs[4:10]
        refs = refs[10:]
    else:
        dq_ref, gkv_ref = refs[:2]
        refs = refs[2:]
    (
    kv_buf,
    part_send,
    part_recv,
    own_part,
    p_scr,
    ds_scr,
    bias,
    g_send,
    g_recv,
    r_send,
    r_recv,
    ) = refs[:11]
    if with_adapters:
        downs, q_act, *rest = refs[11:]
        q_bufs, v_bufs = rest[:10], rest[10:]
    kv_heads = kv_ref.shape[1]
    tok = kv_ref.shape[2]
    repeat = q_ref.shape[1] // kv_heads
    mid = devs // 2
    scaling = HEAD_SIZE ** (-0.5)
    exponent = scaling * math.log2(math.e)
    me = lax.axis_index("ctx")
    p0 = lax.rem(me, devs)
    small = p0 // mid
    big = 1 - small
    ps = lax.rem(p0, mid)

    def ahead(d):
        return lax.rem(me + d, ctx)

    def behind(d):
        return lax.rem(me + ctx - d, ctx)

    barrier = pltpu.get_barrier_semaphore()
    for d in range(1, devs):
        pl.semaphore_signal(barrier, inc=1, device_id={"ctx": ahead(d)}, device_id_type=MESH)
        pl.semaphore_signal(barrier, inc=1, device_id={"ctx": behind(d)}, device_id_type=MESH)
    planes = ctx // devs
    plane = me // devs
    far = range(1, planes) if with_adapters else range(0)
    for j in far:
        pl.semaphore_signal(
            barrier,
            inc=1,
            device_id={"ctx": lax.rem(me + j * devs, ctx)},
            device_id_type=MESH,
        )
    pl.semaphore_wait(barrier, 2 * (devs - 1) + len(far))

    def gather_copy(h, d):
        return pltpu.make_async_remote_copy(
            src_ref=kv_ref.at[h],
            dst_ref=kv_buf.at[h, d],
            send_sem=g_send.at[h, d],
            recv_sem=g_recv.at[h, d],
            device_id={"ctx": ahead(d)},
            device_id_type=MESH,
        )

    def return_copy(h, g, d):
        return pltpu.make_async_remote_copy(
            src_ref=part_send.at[h, g, d],
            dst_ref=part_recv.at[h, g, d],
            send_sem=r_send.at[h, g, d],
            recv_sem=r_recv.at[h, g, d],
            device_id={"ctx": behind(d)},
            device_id_type=MESH,
        )

    for d in range(1, mid):

        @pl.when(ps + d < mid)
        def _():
            gather_copy(small, d).start()

    for d in range(1, devs):

        @pl.when((ps + d >= mid) & (ps + d < devs))
        def _():
            gather_copy(small, d).start()

    for d in range(1, mid):

        @pl.when(ps + d < mid)
        def _():
            gather_copy(big, d).start()

    for h in range(2):
        kv_buf[h, 0] = kv_ref[h]
    for d in range(1, mid):

        @pl.when(d > ps)
        def _():
            kv_buf[small, d] = jnp.zeros(kv_buf.shape[2:], kv_buf.dtype)

        @pl.when(d > ps)
        def _():
            kv_buf[big, mid + d] = jnp.zeros(kv_buf.shape[2:], kv_buf.dtype)

    own_ids = jnp.transpose(
        jnp.broadcast_to(seg_ref[pl.ds(me, 1), :].astype(jnp.float32), (tok, tok))
    )
    rows = lax.broadcasted_iota(jnp.int32, (tok, tok), 0)
    columns = lax.broadcasted_iota(jnp.int32, (tok, tok), 1)
    for d in range(devs):
        ids = seg_ref[pl.ds(behind(d), 1), :].astype(jnp.float32)
        block = jnp.where(own_ids == ids, 0.0, MASKED)
        if d == 0:
            block = jnp.where(columns <= rows, block, MASKED)
        bias[:, d * tok : (d + 1) * tok] = block

    def within(j):
        return lax.rem(p0 + j, devs)

    def scatter_copy(bufs, j):
        part, landed, s_send, s_recv = bufs[0], bufs[1], bufs[4], bufs[5]
        return pltpu.make_async_remote_copy(
            src_ref=part.at[within(j)],
            dst_ref=landed.at[j],
            send_sem=s_send.at[j],
            recv_sem=s_recv.at[j],
            device_id={"ctx": plane * devs + within(j)},
            device_id_type=MESH,
        )

    def plane_copy(bufs, j):
        across, s_send, s_recv = bufs[2], bufs[6], bufs[7]
        return pltpu.make_async_remote_copy(
            src_ref=across.at[plane],
            dst_ref=across.at[plane],
            send_sem=s_send.at[j],
            recv_sem=s_recv.at[j],
            device_id={"ctx": lax.rem(me + j * devs, ctx)},
            device_id_type=MESH,
        )

    def spread_copy(bufs, j):
        whole, s_send, s_recv = bufs[3], bufs[8], bufs[9]
        return pltpu.make_async_remote_copy(
            src_ref=whole.at[p0],
            dst_ref=whole.at[p0],
            send_sem=s_send.at[j],
            recv_sem=s_recv.at[j],
            device_id={"ctx": plane * devs + within(j)},
            device_id_type=MESH,
        )

    def start_scatter(bufs):
        for j in range(1, devs):
            scatter_copy(bufs, j).start()

    def start_planes(bufs):
        total = bufs[0][p0].astype(jnp.float32)
        for j in range(1, devs):
            scatter_copy(bufs, j).wait_recv()
            total = total + bufs[1][j].astype(jnp.float32)
        bufs[2][plane] = total.astype(jnp.bfloat16)
        for j in range(1, planes):
            plane_copy(bufs, j).start()

    def start_spread(bufs):
        for j in range(1, planes):
            plane_copy(bufs, j).wait_recv()
        total = bufs[2][0].astype(jnp.float32)
        for j in range(1, planes):
            total = total + bufs[2][j].astype(jnp.float32)
        bufs[3][p0] = total.astype(jnp.bfloat16)
        for j in range(1, devs):
            spread_copy(bufs, j).start()

    def finish(bufs, down_out, up_out, up_pieces):
        for j in range(1, devs):
            spread_copy(bufs, j).wait_recv()
        width = down_out.shape[1] // devs
        up_width = up_out.shape[1] // up_pieces
        for p in range(devs):
            down_out[:, p * width : (p + 1) * width] = adapter_scale * bufs[3][
                p, :, :width
            ].astype(jnp.float32)
            if p < up_pieces:
                up_out[:, p * up_width : (p + 1) * up_width] = adapter_scale * bufs[3][
                    p, :, width:
                ].astype(jnp.float32)
        for j in range(1, devs):
            scatter_copy(bufs, j).wait_send()
            spread_copy(bufs, j).wait_send()
        for j in range(1, planes):
            plane_copy(bufs, j).wait_send()

    def project_down(bufs, act):
        width = x_ref.shape[1] // devs
        for p in range(devs):
            bufs[0][p, :, :width] = jnp.dot(
                act, x_ref[:, p * width : (p + 1) * width], preferred_element_type=jnp.float32
            ).astype(jnp.bfloat16)

    if with_adapters:
        acts = lax.dot_general(
            down_ref[...], x_ref[...], (((1,), (1,)), ((), ())), preferred_element_type=jnp.float32
        ).astype(jnp.bfloat16)
        downs[...] = acts
        q_act[...] = jnp.zeros_like(q_act)
        rank = q_act.shape[0]
        for p in range(2 * kv_heads, devs):
            v_bufs[0][p, :, x_ref.shape[1] // devs :] = jnp.zeros((rank, HEAD_SIZE), jnp.bfloat16)

    def attend(h, slots, limit):
        keys = slots * tok

        def head_group(g, carry):
            k = kv_buf[h, :slots, g, :, :HEAD_SIZE].reshape(keys, HEAD_SIZE)
            v = kv_buf[h, :slots, g, :, HEAD_SIZE:].reshape(keys, HEAD_SIZE)

            def one_head(r, inner):
                q = q_ref[h, g * repeat + r]
                do = do_ref[h, g * repeat + r]
                s = lax.dot_general(
                    q, k, (((1,), (1,)), ((), ())), preferred_element_type=jnp.float32
                )
                dp = lax.dot_general(
                    do, v, (((1,), (1,)), ((), ())), preferred_element_type=jnp.float32
                )
                at = lax.broadcasted_iota(jnp.int32, (1, keys), 1)
                reach = jnp.where(at < limit * tok, 0.0, MASKED)
                t = s * exponent + (bias[:, :keys] + reach)
                e = jnp.exp2(t - jnp.max(t, axis=1, keepdims=True))
                w = e * (1.0 / jnp.sum(e, axis=1, keepdims=True))
                low = w.astype(jnp.bfloat16)
                dot = jnp.sum(low.astype(jnp.float32) * dp, axis=1, keepdims=True)
                ds = (w * (dp - dot)).astype(jnp.bfloat16)
                at_row = pl.multiple_of(r * tok, tok)
                p_scr[pl.ds(at_row, tok), :keys] = low
                ds_scr[pl.ds(at_row, tok), :keys] = ds
                dq = jnp.dot(ds, k, preferred_element_type=jnp.float32) * scaling
                dq_ref[h, g * repeat + r] = dq.astype(jnp.bfloat16)
                return inner

            lax.fori_loop(0, repeat, one_head, 0, unroll=2)
            if with_adapters:
                dq_all = jnp.concatenate(
                    [dq_ref[h, g * repeat + r] for r in range(repeat)], axis=1
                )
                q_act[...] += lax.dot_general(
                    q_up_ref[h, g],
                    dq_all,
                    (((1,), (1,)), ((), ())),
                    preferred_element_type=jnp.float32,
                )
                up = jnp.dot(downs[:rank], dq_all, preferred_element_type=jnp.float32)
                up = up.astype(jnp.bfloat16)
                width = x_ref.shape[1] // devs
                each = repeat * HEAD_SIZE * 2 * kv_heads // devs
                pieces = repeat * HEAD_SIZE // each
                for i in range(pieces):
                    q_bufs[0][(h * kv_heads + g) * pieces + i, :, width:] = up[
                        :, i * each : (i + 1) * each
                    ]
            q_all = q_ref[h, pl.ds(g * repeat, repeat)].reshape(repeat * tok, HEAD_SIZE)
            do_all = do_ref[h, pl.ds(g * repeat, repeat)].reshape(repeat * tok, HEAD_SIZE)
            dk = lax.dot_general(
                q_all,
                ds_scr[:, :keys],
                (((0,), (0,)), ((), ())),
                preferred_element_type=jnp.float32,
            )
            dv = lax.dot_general(
                do_all,
                p_scr[:, :keys],
                (((0,), (0,)), ((), ())),
                preferred_element_type=jnp.float32,
            )
            for d in range(slots):
                dk_block = jnp.transpose(dk[:, d * tok : (d + 1) * tok]) * scaling
                dv_block = jnp.transpose(dv[:, d * tok : (d + 1) * tok])
                if d == 0:
                    own_part[h, g, :, :HEAD_SIZE] = dk_block
                    own_part[h, g, :, HEAD_SIZE:] = dv_block
                else:
                    part_send[h, g, d, :, :HEAD_SIZE] = dk_block.astype(jnp.bfloat16)
                    part_send[h, g, d, :, HEAD_SIZE:] = dv_block.astype(jnp.bfloat16)
            for d in range(1, slots):

                @pl.when(d < limit)
                def _():
                    return_copy(h, g, d).start()

            return carry

        lax.fori_loop(0, kv_heads, head_group, 0)

    for d in range(1, mid):

        @pl.when(d <= ps)
        def _():
            gather_copy(small, d).wait_recv()

    attend(small, mid, ps + 1)

    for d in range(1, devs):

        @pl.when(d <= ps + mid)
        def _():
            gather_copy(big, d).wait_recv()

    attend(big, devs, ps + mid + 1)

    if with_adapters:
        project_down(q_bufs, q_act[...].astype(jnp.bfloat16))
        start_scatter(q_bufs)

    for d in range(1, devs):
        for g in range(kv_heads):

            @pl.when(ps + d < devs)
            def _():
                return_copy(small, g, d).wait_recv()
                own_part[small, g] = own_part[small, g] + part_recv[small, g, d].astype(
                    jnp.float32
                )

    for d in range(1, mid):
        for g in range(kv_heads):

            @pl.when(ps + d < mid)
            def _():
                return_copy(big, g, d).wait_recv()
                own_part[big, g] = own_part[big, g] + part_recv[big, g, d].astype(jnp.float32)

    gkv_ref[...] = own_part[...].astype(jnp.bfloat16)

    if with_adapters:
        v_act = jnp.zeros(q_act.shape, jnp.float32)
        for h in range(2):
            for g in range(kv_heads):
                gv = gkv_ref[h, g, :, HEAD_SIZE:]
                v_act = v_act + lax.dot_general(
                    v_up_ref[h, g],
                    gv,
                    (((1,), (1,)), ((), ())),
                    preferred_element_type=jnp.float32,
                )
                v_bufs[0][h * kv_heads + g, :, x_ref.shape[1] // devs :] = jnp.dot(
                    downs[rank:], gv, preferred_element_type=jnp.float32
                ).astype(jnp.bfloat16)
        project_down(v_bufs, v_act.astype(jnp.bfloat16))
        start_scatter(v_bufs)
        start_planes(q_bufs)
        start_planes(v_bufs)
        start_spread(q_bufs)
        start_spread(v_bufs)
        finish(q_bufs, qd_out, qu_out, devs)
        finish(v_bufs, vd_out, vu_out, 2 * kv_heads)

    for d in range(1, devs):

        @pl.when(ps + d < devs)
        def _():
            gather_copy(small, d).wait_send()

        @pl.when(d <= ps + mid)
        def _():
            for g in range(kv_heads):
                return_copy(big, g, d).wait_send()

    for d in range(1, mid):

        @pl.when(ps + d < mid)
        def _():
            gather_copy(big, d).wait_send()

        @pl.when(d <= ps)
        def _():
            for g in range(kv_heads):
                return_copy(small, g, d).wait_send()


def attention_backward(q, do, kv, seg, devs, adapters=None):
    heads, tok = q.shape[1], q.shape[2]
    kv_heads = kv.shape[1]
    repeat = heads // kv_heads
    ctx = lax.axis_size("ctx")
    planes = ctx // devs
    bf16, f32 = jnp.bfloat16, jnp.float32
    pair = 2 * HEAD_SIZE
    vmem = pl.BlockSpec(memory_space=pltpu.VMEM)
    operands = (q, do, kv, seg)
    results = [jax.ShapeDtypeStruct(q.shape, bf16), jax.ShapeDtypeStruct(kv.shape, bf16)]
    scratch = [
        pltpu.VMEM((2, devs, kv_heads, tok, pair), bf16),
        pltpu.VMEM((2, kv_heads, devs, tok, pair), bf16),
        pltpu.VMEM((2, kv_heads, devs, tok, pair), bf16),
        pltpu.VMEM((2, kv_heads, tok, pair), f32),
        pltpu.VMEM((repeat * tok, devs * tok), bf16),
        pltpu.VMEM((repeat * tok, devs * tok), bf16),
        pltpu.VMEM((tok, devs * tok), f32),
        pltpu.SemaphoreType.DMA((2, devs)),
        pltpu.SemaphoreType.DMA((2, devs)),
        pltpu.SemaphoreType.DMA((2, kv_heads, devs)),
        pltpu.SemaphoreType.DMA((2, kv_heads, devs)),
    ]
    if adapters is not None:
        operands = operands + adapters
        rank = adapters[1].shape[0] // 2
        width = adapters[0].shape[1]
        q_width, v_width = 2 * heads * HEAD_SIZE, 2 * kv_heads * HEAD_SIZE
        results += [
            jax.ShapeDtypeStruct((rank, n), f32) for n in (width, q_width, width, v_width)
        ]
        scratch += [pltpu.VMEM((2 * rank, tok), bf16), pltpu.VMEM((rank, tok), f32)]
        for columns in ((width + q_width) // devs, width // devs + HEAD_SIZE):
            scratch += [
                pltpu.VMEM((n, rank, columns), bf16) for n in (devs, devs, planes, devs)
            ]
            scratch += [
                pltpu.SemaphoreType.DMA((n,)) for n in (devs, devs, planes, planes, devs, devs)
            ]
    return pl.pallas_call(
        functools.partial(attention_kernel, ctx, devs, adapters is not None),
        out_shape=tuple(results),
        in_specs=[vmem] * len(operands),
        out_specs=(vmem,) * len(results),
        scratch_shapes=scratch,
        compiler_params=pltpu.CompilerParams(
            collective_id=0, has_side_effects=True, vmem_limit_bytes=52 * 1024 * 1024
        ),
        name="attention_backward",
    )(*operands)


def on_device(
    projected_queries,
    projected_keys,
    projected_values,
    output_gradient,
    normed_layer_input,
    segment,
    query_adapter_down,
    query_adapter_up,
    value_adapter_down,
    value_adapter_up,
):
    tok_rows = projected_queries.shape[0]
    query_width = projected_queries.shape[2]
    key_width = projected_keys.shape[2]
    key_value_heads = key_width // HEAD_SIZE
    group_devs = GROUP // tok_rows
    query_heads = query_width // HEAD_SIZE

    def by_head(x, heads):
        return x.reshape(tok_rows, 2, heads, HEAD_SIZE).transpose(1, 2, 0, 3)

    keys_values = jnp.concatenate(
        [by_head(projected_keys, key_value_heads), by_head(projected_values, key_value_heads)],
        axis=3,
    )
    whole_width = lax.axis_size("fsdp") == 1 and 2 * key_value_heads <= group_devs
    adapters = None
    if whole_width:
        rank = query_adapter_up.shape[0]
        adapters = (
            normed_layer_input,
            jnp.concatenate([query_adapter_down, value_adapter_down], axis=0),
            query_adapter_up.reshape(rank, 2, key_value_heads, -1).transpose(1, 2, 0, 3),
            value_adapter_up.reshape(rank, 2, key_value_heads, -1).transpose(1, 2, 0, 3),
        )
    query_grad, pair_grad, *totals = attention_backward(
        by_head(projected_queries, query_heads),
        by_head(output_gradient, query_heads),
        keys_values,
        segment.reshape(-1, tok_rows),
        group_devs,
        adapters,
    )
    grad_query = query_grad.transpose(2, 0, 1, 3).reshape(tok_rows, 2, query_width)
    grad_key = pair_grad[..., :HEAD_SIZE].transpose(2, 0, 1, 3).reshape(tok_rows, 2, key_width)
    grad_value = pair_grad[..., HEAD_SIZE:].transpose(2, 0, 1, 3).reshape(tok_rows, 2, key_width)
    if whole_width:
        return (
            grad_query,
            grad_key,
            grad_value,
            totals[0],
            totals[1].reshape(rank, 2, query_width),
            totals[2],
            totals[3].reshape(rank, 2, key_width),
        )
    adapter_input = lax.psum(
        (
            jnp.dot(normed_layer_input, query_adapter_down.T, preferred_element_type=jnp.float32),
            jnp.dot(normed_layer_input, value_adapter_down.T, preferred_element_type=jnp.float32),
        ),
        "fsdp",
    )
    query_down_part = adapter_input[0].astype(jnp.bfloat16)
    value_down_part = adapter_input[1].astype(jnp.bfloat16)
    query_flattened_rows = grad_query.reshape(tok_rows, -1)
    value_flattened_rows = grad_value.reshape(tok_rows, -1)
    adapter_rank_rows = query_adapter_up.shape[0]
    adapter_output = lax.psum(
        (
            jnp.dot(
                query_flattened_rows,
                query_adapter_up.reshape(adapter_rank_rows, -1).T,
                preferred_element_type=jnp.float32,
            ),
            jnp.dot(
                value_flattened_rows,
                value_adapter_up.reshape(adapter_rank_rows, -1).T,
                preferred_element_type=jnp.float32,
            ),
        ),
        "fsdp",
    )
    query_up_part = adapter_output[0].astype(jnp.bfloat16)
    value_up_part = adapter_output[1].astype(jnp.bfloat16)
    local_down_query = jnp.dot(
        query_up_part.T, normed_layer_input, preferred_element_type=jnp.float32
    )
    local_up_query = jnp.dot(
        query_down_part.T, query_flattened_rows, preferred_element_type=jnp.float32
    ).reshape(adapter_rank_rows, 2, -1)
    local_down_value = jnp.dot(
        value_up_part.T, normed_layer_input, preferred_element_type=jnp.float32
    )
    local_up_value = jnp.dot(
        value_down_part.T, value_flattened_rows, preferred_element_type=jnp.float32
    ).reshape(adapter_rank_rows, 2, -1)
    gradient_totals = lax.psum(
        (local_down_query, local_up_query, local_down_value, local_up_value), "ctx"
    )
    return (
        grad_query,
        grad_key,
        grad_value,
        adapter_scale * gradient_totals[0],
        adapter_scale * gradient_totals[1],
        adapter_scale * gradient_totals[2],
        adapter_scale * gradient_totals[3],
    )


def solution(mesh):
    in_specs = (
        P(("rep", "ctx"), None, "fsdp"),
        P(("rep", "ctx"), None, "fsdp"),
        P(("rep", "ctx"), None, "fsdp"),
        P(("rep", "ctx"), None, "fsdp"),
        P(("rep", "ctx"), "fsdp"),
        P("rep"),
        P(None, "fsdp"),
        P(None, None, "fsdp"),
        P(None, "fsdp"),
        P(None, None, "fsdp"),
    )
    out_specs = (
        P(("rep", "ctx"), None, "fsdp"),
        P(("rep", "ctx"), None, "fsdp"),
        P(("rep", "ctx"), None, "fsdp"),
        P("rep", "fsdp"),
        P("rep", None, "fsdp"),
        P("rep", "fsdp"),
        P("rep", None, "fsdp"),
    )
    return jax.shard_map(
        on_device, mesh=mesh, in_specs=in_specs, out_specs=out_specs, check_vma=False
    )
```

```python
import functools
import math

import jax
import jax.numpy as jnp
from jax import lax
from jax.experimental import pallas as pl
from jax.experimental.pallas import tpu as pltpu
from jax.sharding import PartitionSpec as P

MESH = pl.DeviceIdType.MESH
MASKED = -1e30

QUERY_HEADS = 32
KEY_VALUE_HEADS = 4
HEAD_SIZE = 128
GROUP = 1024


adapter_scale = 2.0


def attention_kernel(
    ctx,
    devs,
    with_adapters,
    q_ref,
    do_ref,
    k_ref,
    v_ref,
    seg_ref,
    *refs,
):
    if with_adapters:
        x_ref, q_down_ref, v_down_ref, q_up_ref, v_up_ref = refs[:5]
        dq_ref, gk_ref, gv_ref, qd_out, qu_out, vd_out, vu_out = refs[5:12]
        refs = refs[12:]
    else:
        dq_ref, gk_ref, gv_ref = refs[:3]
        refs = refs[3:]
    kv_buf, part_send, part_recv, own_part, p_scr, w_scr, bias, g_send, g_recv, r_send, r_recv = (
        refs[:11]
    )
    if with_adapters:
        q_down, v_down, q_up, v_up, q_act = refs[11:16]
        q_bufs, v_bufs = refs[16:26], refs[26:]
    tok = k_ref.shape[1]
    kv_heads = k_ref.shape[2] // HEAD_SIZE
    repeat = q_ref.shape[2] // k_ref.shape[2]
    group_width = repeat * HEAD_SIZE
    mid = devs // 2
    scaling = HEAD_SIZE ** (-0.5)
    exponent = scaling * math.log2(math.e)
    me = lax.axis_index("ctx")
    p0 = lax.rem(me, devs)
    small = p0 // mid
    big = 1 - small
    ps = lax.rem(p0, mid)

    def ahead(d):
        return lax.rem(me + d, ctx)

    def behind(d):
        return lax.rem(me + ctx - d, ctx)

    for h in range(2):
        for g in range(kv_heads):
            lanes = slice(g * HEAD_SIZE, (g + 1) * HEAD_SIZE)
            kv_buf[h, 0, g, :, :HEAD_SIZE] = k_ref[h, :, lanes]
            kv_buf[h, 0, g, :, HEAD_SIZE:] = v_ref[h, :, lanes]

    barrier = pltpu.get_barrier_semaphore()
    for d in range(1, devs):
        pl.semaphore_signal(barrier, inc=1, device_id={"ctx": ahead(d)}, device_id_type=MESH)
        pl.semaphore_signal(barrier, inc=1, device_id={"ctx": behind(d)}, device_id_type=MESH)
    planes = ctx // devs
    plane = me // devs
    far = range(1, planes) if with_adapters else range(0)
    for j in far:
        pl.semaphore_signal(
            barrier,
            inc=1,
            device_id={"ctx": lax.rem(me + j * devs, ctx)},
            device_id_type=MESH,
        )
    pl.semaphore_wait(barrier, 2 * (devs - 1) + len(far))

    def gather_copy(h, d):
        return pltpu.make_async_remote_copy(
            src_ref=kv_buf.at[h, 0],
            dst_ref=kv_buf.at[h, d],
            send_sem=g_send.at[h, d],
            recv_sem=g_recv.at[h, d],
            device_id={"ctx": ahead(d)},
            device_id_type=MESH,
        )

    def return_copy(which, h, g, d):
        return pltpu.make_async_remote_copy(
            src_ref=part_send.at[which, h, g, d],
            dst_ref=part_recv.at[which, h, g, d],
            send_sem=r_send.at[which, h, g, d],
            recv_sem=r_recv.at[which, h, g, d],
            device_id={"ctx": behind(d)},
            device_id_type=MESH,
        )

    for d in range(1, mid):

        @pl.when(ps + d < mid)
        def _():
            gather_copy(small, d).start()

    for d in range(1, devs):

        @pl.when((ps + d >= mid) & (ps + d < devs))
        def _():
            gather_copy(small, d).start()

    for d in range(1, mid):

        @pl.when(ps + d < mid)
        def _():
            gather_copy(big, d).start()

    for d in range(1, mid):

        @pl.when(d > ps)
        def _():
            kv_buf[small, d] = jnp.zeros(kv_buf.shape[2:], kv_buf.dtype)

        @pl.when(d > ps)
        def _():
            kv_buf[big, mid + d] = jnp.zeros(kv_buf.shape[2:], kv_buf.dtype)

    own_ids = jnp.transpose(
        jnp.broadcast_to(seg_ref[pl.ds(me, 1), :].astype(jnp.float32), (tok, tok))
    )
    rows = lax.broadcasted_iota(jnp.int32, (tok, tok), 0)
    columns = lax.broadcasted_iota(jnp.int32, (tok, tok), 1)
    for d in range(devs):
        ids = seg_ref[pl.ds(behind(d), 1), :].astype(jnp.float32)
        block = jnp.where(own_ids == ids, 0.0, MASKED)
        if d == 0:
            block = jnp.where(columns <= rows, block, MASKED)
        bias[1, :, d * tok : (d + 1) * tok] = jnp.where(d <= ps + mid, block, MASKED)
        if d < mid:
            bias[0, :, d * tok : (d + 1) * tok] = jnp.where(d <= ps, block, MASKED)

    def within(j):
        return lax.rem(p0 + j, devs)

    def scatter_copy(bufs, j):
        part, landed, s_send, s_recv = bufs[0], bufs[1], bufs[4], bufs[5]
        return pltpu.make_async_remote_copy(
            src_ref=part.at[within(j)],
            dst_ref=landed.at[j],
            send_sem=s_send.at[j],
            recv_sem=s_recv.at[j],
            device_id={"ctx": plane * devs + within(j)},
            device_id_type=MESH,
        )

    def plane_copy(bufs, j):
        across, s_send, s_recv = bufs[2], bufs[6], bufs[7]
        return pltpu.make_async_remote_copy(
            src_ref=across.at[plane],
            dst_ref=across.at[plane],
            send_sem=s_send.at[j],
            recv_sem=s_recv.at[j],
            device_id={"ctx": lax.rem(me + j * devs, ctx)},
            device_id_type=MESH,
        )

    def spread_copy(bufs, j):
        whole, s_send, s_recv = bufs[3], bufs[8], bufs[9]
        return pltpu.make_async_remote_copy(
            src_ref=whole.at[p0],
            dst_ref=whole.at[p0],
            send_sem=s_send.at[j],
            recv_sem=s_recv.at[j],
            device_id={"ctx": plane * devs + within(j)},
            device_id_type=MESH,
        )

    def start_scatter(bufs):
        for j in range(1, devs):
            scatter_copy(bufs, j).start()

    def start_planes(bufs):
        total = bufs[0][p0].astype(jnp.float32)
        for j in range(1, devs):
            scatter_copy(bufs, j).wait_recv()
            total = total + bufs[1][j].astype(jnp.float32)
        bufs[2][plane] = total.astype(jnp.bfloat16)
        for j in range(1, planes):
            plane_copy(bufs, j).start()

    def start_spread(bufs):
        for j in range(1, planes):
            plane_copy(bufs, j).wait_recv()
        total = bufs[2][0].astype(jnp.float32)
        for j in range(1, planes):
            total = total + bufs[2][j].astype(jnp.float32)
        bufs[3][p0] = total.astype(jnp.bfloat16)
        for j in range(1, devs):
            spread_copy(bufs, j).start()

    def finish(bufs, down_out, up_out, up_pieces):
        for j in range(1, devs):
            spread_copy(bufs, j).wait_recv()
        width = down_out.shape[1] // devs
        up_width = 2 * up_out.shape[2] // up_pieces
        for p in range(devs):
            down_out[:, p * width : (p + 1) * width] = adapter_scale * bufs[3][
                p, :, :width
            ].astype(jnp.float32)
            if p < up_pieces:
                h, at = p // (up_pieces // 2), p % (up_pieces // 2)
                up_out[:, h, at * up_width : (at + 1) * up_width] = adapter_scale * bufs[3][
                    p, :, width:
                ].astype(jnp.float32)
        for j in range(1, devs):
            scatter_copy(bufs, j).wait_send()
            spread_copy(bufs, j).wait_send()
        for j in range(1, planes):
            plane_copy(bufs, j).wait_send()

    def project_down(bufs, act):
        width = x_ref.shape[1] // devs
        for p in range(devs):
            bufs[0][p, :, :width] = jnp.dot(
                act, x_ref[:, p * width : (p + 1) * width], preferred_element_type=jnp.float32
            ).astype(jnp.bfloat16)

    if with_adapters:
        for source, act in ((q_down_ref, q_down), (v_down_ref, v_down)):
            act[...] = lax.dot_general(
                source[...],
                x_ref[...],
                (((1,), (1,)), ((), ())),
                preferred_element_type=jnp.float32,
            ).astype(jnp.bfloat16)
        for h in range(2):
            q_up[h] = q_up_ref[:, h, :]
            v_up[h] = v_up_ref[:, h, :]
        q_act[...] = jnp.zeros_like(q_act)
        rank = q_act.shape[0]
        for p in range(2 * kv_heads, devs):
            v_bufs[0][p, :, x_ref.shape[1] // devs :] = jnp.zeros((rank, HEAD_SIZE), jnp.bfloat16)

    def stacked(ref, h, g):
        return jnp.concatenate(
            [
                ref[h, :, g * group_width + r * HEAD_SIZE : g * group_width + (r + 1) * HEAD_SIZE]
                for r in range(repeat)
            ],
            axis=0,
        )

    def send_parts(which, total, h, g, slots, limit):
        for d in range(slots):
            block = jnp.transpose(total[:, d * tok : (d + 1) * tok])
            if d == 0:
                own_part[which, h, g] = block
            else:
                part_send[which, h, g, d] = block.astype(jnp.bfloat16)
        for d in range(1, slots):

            @pl.when(d < limit)
            def _():
                return_copy(which, h, g, d).start()

    def probabilities(h, g, slots, limit):
        keys = slots * tok
        k = kv_buf[h, :slots, g, :, :HEAD_SIZE].reshape(keys, HEAD_SIZE)

        def one_head(r, inner):
            lanes = pl.ds(pl.multiple_of(g * group_width + r * HEAD_SIZE, HEAD_SIZE), HEAD_SIZE)
            at = pl.ds(pl.multiple_of(r * tok, tok), tok)
            s = lax.dot_general(
                q_ref[h, :, lanes],
                k,
                (((1,), (1,)), ((), ())),
                preferred_element_type=jnp.float32,
            )
            t = s * exponent + bias[int(slots == devs), :, :keys]
            e = jnp.exp2(t - jnp.max(t, axis=1, keepdims=True))
            w = e * (1.0 / jnp.sum(e, axis=1, keepdims=True))
            w_scr[g, at, :keys] = w
            p_scr[at, :keys] = w.astype(jnp.bfloat16)
            return inner

        lax.fori_loop(0, repeat, one_head, 0, unroll=2)
        dv = lax.dot_general(
            stacked(do_ref, h, g),
            p_scr[:, :keys],
            (((0,), (0,)), ((), ())),
            preferred_element_type=jnp.float32,
        )
        send_parts(1, dv, h, g, slots, limit)

    def score_gradients(h, g, slots, limit):
        keys = slots * tok
        k = kv_buf[h, :slots, g, :, :HEAD_SIZE].reshape(keys, HEAD_SIZE)
        v = kv_buf[h, :slots, g, :, HEAD_SIZE:].reshape(keys, HEAD_SIZE)

        def one_head(r, inner):
            lanes = pl.ds(pl.multiple_of(g * group_width + r * HEAD_SIZE, HEAD_SIZE), HEAD_SIZE)
            at = pl.ds(pl.multiple_of(r * tok, tok), tok)
            dp = lax.dot_general(
                do_ref[h, :, lanes],
                v,
                (((1,), (1,)), ((), ())),
                preferred_element_type=jnp.float32,
            )
            w = w_scr[g, at, :keys]
            low = w.astype(jnp.bfloat16).astype(jnp.float32)
            dot = jnp.sum(low * dp, axis=1, keepdims=True)
            ds = (w * (dp - dot)).astype(jnp.bfloat16)
            p_scr[at, :keys] = ds
            dq = jnp.dot(ds, k, preferred_element_type=jnp.float32) * scaling
            dq_ref[h, :, lanes] = dq.astype(jnp.bfloat16)
            return inner

        lax.fori_loop(0, repeat, one_head, 0, unroll=2)
        if with_adapters:
            lanes = slice(g * group_width, (g + 1) * group_width)
            dq_all = dq_ref[h, :, lanes]
            q_act[...] += lax.dot_general(
                q_up[h, :, lanes],
                dq_all,
                (((1,), (1,)), ((), ())),
                preferred_element_type=jnp.float32,
            )
            up = jnp.dot(q_down[...], dq_all, preferred_element_type=jnp.float32)
            up = up.astype(jnp.bfloat16)
            width = x_ref.shape[1] // devs
            each = group_width * 2 * kv_heads // devs
            pieces = group_width // each
            for i in range(pieces):
                q_bufs[0][(h * kv_heads + g) * pieces + i, :, width:] = up[
                    :, i * each : (i + 1) * each
                ]
        dk = lax.dot_general(
            stacked(q_ref, h, g),
            p_scr[:, :keys],
            (((0,), (0,)), ((), ())),
            preferred_element_type=jnp.float32,
        )
        send_parts(0, dk * scaling, h, g, slots, limit)

    def collect(which, out_ref):
        for d in range(1, devs):
            for g in range(kv_heads):

                @pl.when(ps + d < devs)
                def _():
                    return_copy(which, small, g, d).wait_recv()
                    own_part[which, small, g] += part_recv[which, small, g, d].astype(jnp.float32)

        for d in range(1, mid):
            for g in range(kv_heads):

                @pl.when(ps + d < mid)
                def _():
                    return_copy(which, big, g, d).wait_recv()
                    own_part[which, big, g] += part_recv[which, big, g, d].astype(jnp.float32)

        for h in range(2):
            for g in range(kv_heads):
                out_ref[h, :, g * HEAD_SIZE : (g + 1) * HEAD_SIZE] = own_part[which, h, g].astype(
                    jnp.bfloat16
                )

    def value_adapter():
        v_act = jnp.zeros(q_act.shape, jnp.float32)
        for h in range(2):
            v_act = v_act + lax.dot_general(
                v_up[h], gv_ref[h], (((1,), (1,)), ((), ())), preferred_element_type=jnp.float32
            )
            up = jnp.dot(v_down[...], gv_ref[h], preferred_element_type=jnp.float32)
            for g in range(kv_heads):
                v_bufs[0][h * kv_heads + g, :, x_ref.shape[1] // devs :] = up[
                    :, g * HEAD_SIZE : (g + 1) * HEAD_SIZE
                ].astype(jnp.bfloat16)
        project_down(v_bufs, v_act.astype(jnp.bfloat16))
        start_scatter(v_bufs)

    for d in range(1, mid):

        @pl.when(d <= ps)
        def _():
            gather_copy(small, d).wait_recv()

    for g in range(kv_heads):
        probabilities(small, g, mid, ps + 1)
    for g in range(kv_heads):
        score_gradients(small, g, mid, ps + 1)

    for d in range(1, devs):

        @pl.when(d <= ps + mid)
        def _():
            gather_copy(big, d).wait_recv()

    for g in range(kv_heads):
        probabilities(big, g, devs, ps + mid + 1)
    for g in range(kv_heads):
        score_gradients(big, g, devs, ps + mid + 1)
        if g == 0:
            collect(1, gv_ref)
            if with_adapters:
                value_adapter()

    if with_adapters:
        start_planes(v_bufs)
        project_down(q_bufs, q_act[...].astype(jnp.bfloat16))
        start_scatter(q_bufs)
        start_spread(v_bufs)
    collect(0, gk_ref)
    if with_adapters:
        start_planes(q_bufs)
        finish(v_bufs, vd_out, vu_out, 2 * kv_heads)
        start_spread(q_bufs)
        finish(q_bufs, qd_out, qu_out, devs)

    for d in range(1, devs):

        @pl.when(ps + d < devs)
        def _():
            gather_copy(small, d).wait_send()

        @pl.when(d <= ps + mid)
        def _():
            for which in range(2):
                for g in range(kv_heads):
                    return_copy(which, big, g, d).wait_send()

    for d in range(1, mid):

        @pl.when(ps + d < mid)
        def _():
            gather_copy(big, d).wait_send()

        @pl.when(d <= ps)
        def _():
            for which in range(2):
                for g in range(kv_heads):
                    return_copy(which, small, g, d).wait_send()


def attention_backward(q, do, k, v, seg, devs, adapters=None):
    tok, width = q.shape[1], q.shape[2]
    kv_heads = k.shape[2] // HEAD_SIZE
    repeat = width // k.shape[2]
    ctx = lax.axis_size("ctx")
    planes = ctx // devs
    bf16, f32 = jnp.bfloat16, jnp.float32
    vmem = pl.BlockSpec(memory_space=pltpu.VMEM)
    operands = (q, do, k, v, seg)
    results = [jax.ShapeDtypeStruct(a.shape, bf16) for a in (q, k, v)]
    scratch = [
        pltpu.VMEM((2, devs, kv_heads, tok, 2 * HEAD_SIZE), bf16),
        pltpu.VMEM((2, 2, kv_heads, devs, tok, HEAD_SIZE), bf16),
        pltpu.VMEM((2, 2, kv_heads, devs, tok, HEAD_SIZE), bf16),
        pltpu.VMEM((2, 2, kv_heads, tok, HEAD_SIZE), f32),
        pltpu.VMEM((repeat * tok, devs * tok), bf16),
        pltpu.VMEM((kv_heads, repeat * tok, devs * tok), f32),
        pltpu.VMEM((2, tok, devs * tok), f32),
        pltpu.SemaphoreType.DMA((2, devs)),
        pltpu.SemaphoreType.DMA((2, devs)),
        pltpu.SemaphoreType.DMA((2, 2, kv_heads, devs)),
        pltpu.SemaphoreType.DMA((2, 2, kv_heads, devs)),
    ]
    if adapters is not None:
        operands = operands + adapters
        x, q_down, v_down, q_up, v_up = adapters
        rank = q_down.shape[0]
        results += [jax.ShapeDtypeStruct(a.shape, f32) for a in (q_down, q_up, v_down, v_up)]
        scratch += [
            pltpu.VMEM((rank, tok), bf16),
            pltpu.VMEM((rank, tok), bf16),
            pltpu.VMEM((2, rank, q.shape[2]), bf16),
            pltpu.VMEM((2, rank, k.shape[2]), bf16),
            pltpu.VMEM((rank, tok), f32),
        ]
        for columns in ((x.shape[1] + 2 * width) // devs, x.shape[1] // devs + HEAD_SIZE):
            scratch += [
                pltpu.VMEM((n, rank, columns), bf16) for n in (devs, devs, planes, devs)
            ]
            scratch += [
                pltpu.SemaphoreType.DMA((n,)) for n in (devs, devs, planes, planes, devs, devs)
            ]
    return pl.pallas_call(
        functools.partial(attention_kernel, ctx, devs, adapters is not None),
        out_shape=tuple(results),
        in_specs=[vmem] * len(operands),
        out_specs=(vmem,) * len(results),
        scratch_shapes=scratch,
        compiler_params=pltpu.CompilerParams(
            collective_id=0, has_side_effects=True, vmem_limit_bytes=52 * 1024 * 1024
        ),
        name="attention_backward",
    )(*operands)


def on_device(
    projected_queries,
    projected_keys,
    projected_values,
    output_gradient,
    normed_layer_input,
    segment,
    query_adapter_down,
    query_adapter_up,
    value_adapter_down,
    value_adapter_up,
):
    tok_rows = projected_queries.shape[0]
    query_width = projected_queries.shape[2]
    key_width = projected_keys.shape[2]
    key_value_heads = key_width // HEAD_SIZE
    group_devs = GROUP // tok_rows
    whole_width = lax.axis_size("fsdp") == 1 and 2 * key_value_heads <= group_devs
    adapters = None
    if whole_width:
        adapters = (
            normed_layer_input,
            query_adapter_down,
            value_adapter_down,
            query_adapter_up,
            value_adapter_up,
        )
    query_grad, key_grad, value_grad, *totals = attention_backward(
        projected_queries.transpose(1, 0, 2),
        output_gradient.transpose(1, 0, 2),
        projected_keys.transpose(1, 0, 2),
        projected_values.transpose(1, 0, 2),
        segment.reshape(-1, tok_rows),
        group_devs,
        adapters,
    )
    grad_query = query_grad.transpose(1, 0, 2)
    grad_key = key_grad.transpose(1, 0, 2)
    grad_value = value_grad.transpose(1, 0, 2)
    if whole_width:
        return (grad_query, grad_key, grad_value, *totals)
    adapter_input = lax.psum(
        (
            jnp.dot(normed_layer_input, query_adapter_down.T, preferred_element_type=jnp.float32),
            jnp.dot(normed_layer_input, value_adapter_down.T, preferred_element_type=jnp.float32),
        ),
        "fsdp",
    )
    query_down_part = adapter_input[0].astype(jnp.bfloat16)
    value_down_part = adapter_input[1].astype(jnp.bfloat16)
    query_flattened_rows = grad_query.reshape(tok_rows, -1)
    value_flattened_rows = grad_value.reshape(tok_rows, -1)
    adapter_rank_rows = query_adapter_up.shape[0]
    adapter_output = lax.psum(
        (
            jnp.dot(
                query_flattened_rows,
                query_adapter_up.reshape(adapter_rank_rows, -1).T,
                preferred_element_type=jnp.float32,
            ),
            jnp.dot(
                value_flattened_rows,
                value_adapter_up.reshape(adapter_rank_rows, -1).T,
                preferred_element_type=jnp.float32,
            ),
        ),
        "fsdp",
    )
    query_up_part = adapter_output[0].astype(jnp.bfloat16)
    value_up_part = adapter_output[1].astype(jnp.bfloat16)
    local_down_query = jnp.dot(
        query_up_part.T, normed_layer_input, preferred_element_type=jnp.float32
    )
    local_up_query = jnp.dot(
        query_down_part.T, query_flattened_rows, preferred_element_type=jnp.float32
    ).reshape(adapter_rank_rows, 2, -1)
    local_down_value = jnp.dot(
        value_up_part.T, normed_layer_input, preferred_element_type=jnp.float32
    )
    local_up_value = jnp.dot(
        value_down_part.T, value_flattened_rows, preferred_element_type=jnp.float32
    ).reshape(adapter_rank_rows, 2, -1)
    gradient_totals = lax.psum(
        (local_down_query, local_up_query, local_down_value, local_up_value), "ctx"
    )
    return (
        grad_query,
        grad_key,
        grad_value,
        adapter_scale * gradient_totals[0],
        adapter_scale * gradient_totals[1],
        adapter_scale * gradient_totals[2],
        adapter_scale * gradient_totals[3],
    )


def solution(mesh):
    in_specs = (
        P(("rep", "ctx"), None, "fsdp"),
        P(("rep", "ctx"), None, "fsdp"),
        P(("rep", "ctx"), None, "fsdp"),
        P(("rep", "ctx"), None, "fsdp"),
        P(("rep", "ctx"), "fsdp"),
        P("rep"),
        P(None, "fsdp"),
        P(None, None, "fsdp"),
        P(None, "fsdp"),
        P(None, None, "fsdp"),
    )
    out_specs = (
        P(("rep", "ctx"), None, "fsdp"),
        P(("rep", "ctx"), None, "fsdp"),
        P(("rep", "ctx"), None, "fsdp"),
        P("rep", "fsdp"),
        P("rep", None, "fsdp"),
        P("rep", "fsdp"),
        P("rep", None, "fsdp"),
    )
    return jax.shard_map(
        on_device, mesh=mesh, in_specs=in_specs, out_specs=out_specs, check_vma=False
    )
```

```python
import functools
import math

import jax
import jax.numpy as jnp
from jax import lax
from jax.experimental import pallas as pl
from jax.experimental.pallas import tpu as pltpu
from jax.sharding import PartitionSpec as P

MESH = pl.DeviceIdType.MESH
MASKED = -1e30

QUERY_HEADS = 32
KEY_VALUE_HEADS = 4
HEAD_SIZE = 128
GROUP = 1024


adapter_scale = 2.0


def attention_kernel(
    ctx,
    devs,
    with_adapters,
    q_ref,
    do_ref,
    k_ref,
    v_ref,
    seg_ref,
    *refs,
):
    if with_adapters:
        x_ref, q_down_ref, v_down_ref, q_up_ref, v_up_ref = refs[:5]
        dq_ref, gk_ref, gv_ref, qd_out, qu_out, vd_out, vu_out = refs[5:12]
        refs = refs[12:]
    else:
        dq_ref, gk_ref, gv_ref = refs[:3]
        refs = refs[3:]
    kv_buf, part_send, part_recv, own_part, p_scr, w_scr, bias, g_send, g_recv, r_send, r_recv = (
        refs[:11]
    )
    if with_adapters:
        q_down, v_down, q_up, v_up, q_act = refs[11:16]
        q_bufs, v_bufs = refs[16:26], refs[26:]
    tok = k_ref.shape[1]
    kv_heads = k_ref.shape[2] // HEAD_SIZE
    repeat = q_ref.shape[2] // k_ref.shape[2]
    group_width = repeat * HEAD_SIZE
    mid = devs // 2
    scaling = HEAD_SIZE ** (-0.5)
    exponent = scaling * math.log2(math.e)
    me = lax.axis_index("ctx")
    p0 = lax.rem(me, devs)
    small = p0 // mid
    big = 1 - small
    ps = lax.rem(p0, mid)

    def ahead(d):
        return lax.rem(me + d, ctx)

    def behind(d):
        return lax.rem(me + ctx - d, ctx)

    for h in range(2):
        for g in range(kv_heads):
            lanes = slice(g * HEAD_SIZE, (g + 1) * HEAD_SIZE)
            kv_buf[h, 0, g, :, :HEAD_SIZE] = k_ref[h, :, lanes]
            kv_buf[h, 0, g, :, HEAD_SIZE:] = v_ref[h, :, lanes]

    barrier = pltpu.get_barrier_semaphore()
    for d in range(1, devs):
        pl.semaphore_signal(barrier, inc=1, device_id={"ctx": ahead(d)}, device_id_type=MESH)
        pl.semaphore_signal(barrier, inc=1, device_id={"ctx": behind(d)}, device_id_type=MESH)
    planes = ctx // devs
    plane = me // devs
    far = range(1, planes) if with_adapters else range(0)
    for j in far:
        pl.semaphore_signal(
            barrier,
            inc=1,
            device_id={"ctx": lax.rem(me + j * devs, ctx)},
            device_id_type=MESH,
        )
    pl.semaphore_wait(barrier, 2 * (devs - 1) + len(far))

    def gather_copy(h, d):
        return pltpu.make_async_remote_copy(
            src_ref=kv_buf.at[h, 0],
            dst_ref=kv_buf.at[h, d],
            send_sem=g_send.at[h, d],
            recv_sem=g_recv.at[h, d],
            device_id={"ctx": ahead(d)},
            device_id_type=MESH,
        )

    def return_copy(which, h, g, d):
        return pltpu.make_async_remote_copy(
            src_ref=part_send.at[which, h, g, d],
            dst_ref=part_recv.at[which, h, g, d],
            send_sem=r_send.at[which, h, g, d],
            recv_sem=r_recv.at[which, h, g, d],
            device_id={"ctx": behind(d)},
            device_id_type=MESH,
        )

    for d in range(1, mid):

        @pl.when(ps + d < mid)
        def _():
            gather_copy(small, d).start()

    for d in range(1, devs):

        @pl.when((ps + d >= mid) & (ps + d < devs))
        def _():
            gather_copy(small, d).start()

    for d in range(1, mid):

        @pl.when(ps + d < mid)
        def _():
            gather_copy(big, d).start()

    for d in range(1, mid):

        @pl.when(d > ps)
        def _():
            kv_buf[small, d] = jnp.zeros(kv_buf.shape[2:], kv_buf.dtype)

        @pl.when(d > ps)
        def _():
            kv_buf[big, mid + d] = jnp.zeros(kv_buf.shape[2:], kv_buf.dtype)

    own_ids = jnp.transpose(
        jnp.broadcast_to(seg_ref[pl.ds(me, 1), :].astype(jnp.float32), (tok, tok))
    )
    rows = lax.broadcasted_iota(jnp.int32, (tok, tok), 0)
    columns = lax.broadcasted_iota(jnp.int32, (tok, tok), 1)
    for d in range(devs):
        ids = seg_ref[pl.ds(behind(d), 1), :].astype(jnp.float32)
        block = jnp.where(own_ids == ids, 0.0, MASKED)
        if d == 0:
            block = jnp.where(columns <= rows, block, MASKED)
        bias[1, :, d * tok : (d + 1) * tok] = jnp.where(d <= ps + mid, block, MASKED)
        if d < mid:
            bias[0, :, d * tok : (d + 1) * tok] = jnp.where(d <= ps, block, MASKED)

    def within(j):
        return lax.rem(p0 + j, devs)

    def scatter_copy(bufs, j):
        part, landed, s_send, s_recv = bufs[0], bufs[1], bufs[4], bufs[5]
        return pltpu.make_async_remote_copy(
            src_ref=part.at[within(j)],
            dst_ref=landed.at[j],
            send_sem=s_send.at[j],
            recv_sem=s_recv.at[j],
            device_id={"ctx": plane * devs + within(j)},
            device_id_type=MESH,
        )

    def plane_copy(bufs, j):
        across, s_send, s_recv = bufs[2], bufs[6], bufs[7]
        return pltpu.make_async_remote_copy(
            src_ref=across.at[plane],
            dst_ref=across.at[plane],
            send_sem=s_send.at[j],
            recv_sem=s_recv.at[j],
            device_id={"ctx": lax.rem(me + j * devs, ctx)},
            device_id_type=MESH,
        )

    def spread_copy(bufs, j):
        whole, s_send, s_recv = bufs[3], bufs[8], bufs[9]
        return pltpu.make_async_remote_copy(
            src_ref=whole.at[p0],
            dst_ref=whole.at[p0],
            send_sem=s_send.at[j],
            recv_sem=s_recv.at[j],
            device_id={"ctx": plane * devs + within(j)},
            device_id_type=MESH,
        )

    def start_scatter(bufs):
        for j in range(1, devs):
            scatter_copy(bufs, j).start()

    def start_planes(bufs):
        total = bufs[0][p0].astype(jnp.float32)
        for j in range(1, devs):
            scatter_copy(bufs, j).wait_recv()
            total = total + bufs[1][j].astype(jnp.float32)
        bufs[2][plane] = total.astype(jnp.bfloat16)
        for j in range(1, planes):
            plane_copy(bufs, j).start()

    def start_spread(bufs):
        for j in range(1, planes):
            plane_copy(bufs, j).wait_recv()
        total = bufs[2][0].astype(jnp.float32)
        for j in range(1, planes):
            total = total + bufs[2][j].astype(jnp.float32)
        bufs[3][p0] = total.astype(jnp.bfloat16)
        for j in range(1, devs):
            spread_copy(bufs, j).start()

    def finish(bufs, down_out, up_out, up_pieces):
        for j in range(1, devs):
            spread_copy(bufs, j).wait_recv()
        width = down_out.shape[1] // devs
        up_width = 2 * up_out.shape[2] // up_pieces
        for p in range(devs):
            down_out[:, p * width : (p + 1) * width] = adapter_scale * bufs[3][
                p, :, :width
            ].astype(jnp.float32)
            if p < up_pieces:
                h, at = p // (up_pieces // 2), p % (up_pieces // 2)
                up_out[:, h, at * up_width : (at + 1) * up_width] = adapter_scale * bufs[3][
                    p, :, width:
                ].astype(jnp.float32)
        for j in range(1, devs):
            scatter_copy(bufs, j).wait_send()
            spread_copy(bufs, j).wait_send()
        for j in range(1, planes):
            plane_copy(bufs, j).wait_send()

    def project_down(bufs, act):
        width = x_ref.shape[1] // devs
        for p in range(devs):
            bufs[0][p, :, :width] = jnp.dot(
                act, x_ref[:, p * width : (p + 1) * width], preferred_element_type=jnp.float32
            ).astype(jnp.bfloat16)

    if with_adapters:
        for source, act in ((q_down_ref, q_down), (v_down_ref, v_down)):
            act[...] = lax.dot_general(
                source[...],
                x_ref[...],
                (((1,), (1,)), ((), ())),
                preferred_element_type=jnp.float32,
            ).astype(jnp.bfloat16)
        for h in range(2):
            q_up[h] = q_up_ref[:, h, :]
            v_up[h] = v_up_ref[:, h, :]
        q_act[...] = jnp.zeros_like(q_act)
        rank = q_act.shape[0]
        for p in range(2 * kv_heads, devs):
            v_bufs[0][p, :, x_ref.shape[1] // devs :] = jnp.zeros((rank, HEAD_SIZE), jnp.bfloat16)

    def stacked(ref, h, g):
        return jnp.concatenate(
            [
                ref[h, :, g * group_width + r * HEAD_SIZE : g * group_width + (r + 1) * HEAD_SIZE]
                for r in range(repeat)
            ],
            axis=0,
        )

    def send_parts(which, total, h, g, slots, limit):
        for d in range(slots):
            block = jnp.transpose(total[:, d * tok : (d + 1) * tok])
            if d == 0:
                own_part[which, h, g] = block
            else:
                part_send[which, h, g, d] = block.astype(jnp.bfloat16)
        for d in range(1, slots):

            @pl.when(d < limit)
            def _():
                return_copy(which, h, g, d).start()

    def probabilities(h, g, slots, limit):
        keys = slots * tok
        k = kv_buf[h, :slots, g, :, :HEAD_SIZE].reshape(keys, HEAD_SIZE)

        def one_head(r, inner):
            lanes = pl.ds(pl.multiple_of(g * group_width + r * HEAD_SIZE, HEAD_SIZE), HEAD_SIZE)
            at = pl.ds(pl.multiple_of(r * tok, tok), tok)
            s = lax.dot_general(
                q_ref[h, :, lanes],
                k,
                (((1,), (1,)), ((), ())),
                preferred_element_type=jnp.float32,
            )
            t = s * exponent + bias[int(slots == devs), :, :keys]
            e = jnp.exp2(t - jnp.max(t, axis=1, keepdims=True))
            w = e * (1.0 / jnp.sum(e, axis=1, keepdims=True))
            w_scr[g, at, :keys] = w
            p_scr[at, :keys] = w.astype(jnp.bfloat16)
            return inner

        lax.fori_loop(0, repeat, one_head, 0, unroll=8)
        dv = lax.dot_general(
            stacked(do_ref, h, g),
            p_scr[:, :keys],
            (((0,), (0,)), ((), ())),
            preferred_element_type=jnp.float32,
        )
        send_parts(1, dv, h, g, slots, limit)

    def score_gradients(h, g, slots, limit):
        keys = slots * tok
        k = kv_buf[h, :slots, g, :, :HEAD_SIZE].reshape(keys, HEAD_SIZE)
        v = kv_buf[h, :slots, g, :, HEAD_SIZE:].reshape(keys, HEAD_SIZE)

        def one_head(r, inner):
            lanes = pl.ds(pl.multiple_of(g * group_width + r * HEAD_SIZE, HEAD_SIZE), HEAD_SIZE)
            at = pl.ds(pl.multiple_of(r * tok, tok), tok)
            dp = lax.dot_general(
                do_ref[h, :, lanes],
                v,
                (((1,), (1,)), ((), ())),
                preferred_element_type=jnp.float32,
            )
            w = w_scr[g, at, :keys]
            low = w.astype(jnp.bfloat16).astype(jnp.float32)
            dot = jnp.sum(low * dp, axis=1, keepdims=True)
            ds = (w * (dp - dot)).astype(jnp.bfloat16)
            p_scr[at, :keys] = ds
            dq = jnp.dot(ds, k, preferred_element_type=jnp.float32) * scaling
            dq_ref[h, :, lanes] = dq.astype(jnp.bfloat16)
            return inner

        lax.fori_loop(0, repeat, one_head, 0, unroll=8)
        if with_adapters:
            lanes = slice(g * group_width, (g + 1) * group_width)
            dq_all = dq_ref[h, :, lanes]
            q_act[...] += lax.dot_general(
                q_up[h, :, lanes],
                dq_all,
                (((1,), (1,)), ((), ())),
                preferred_element_type=jnp.float32,
            )
            up = jnp.dot(q_down[...], dq_all, preferred_element_type=jnp.float32)
            up = up.astype(jnp.bfloat16)
            width = x_ref.shape[1] // devs
            each = group_width * 2 * kv_heads // devs
            pieces = group_width // each
            for i in range(pieces):
                q_bufs[0][(h * kv_heads + g) * pieces + i, :, width:] = up[
                    :, i * each : (i + 1) * each
                ]
        dk = lax.dot_general(
            stacked(q_ref, h, g),
            p_scr[:, :keys],
            (((0,), (0,)), ((), ())),
            preferred_element_type=jnp.float32,
        )
        send_parts(0, dk * scaling, h, g, slots, limit)

    def collect(which, out_ref):
        for d in range(1, devs):
            for g in range(kv_heads):

                @pl.when(ps + d < devs)
                def _():
                    return_copy(which, small, g, d).wait_recv()
                    own_part[which, small, g] += part_recv[which, small, g, d].astype(jnp.float32)

        for d in range(1, mid):
            for g in range(kv_heads):

                @pl.when(ps + d < mid)
                def _():
                    return_copy(which, big, g, d).wait_recv()
                    own_part[which, big, g] += part_recv[which, big, g, d].astype(jnp.float32)

        for h in range(2):
            for g in range(kv_heads):
                out_ref[h, :, g * HEAD_SIZE : (g + 1) * HEAD_SIZE] = own_part[which, h, g].astype(
                    jnp.bfloat16
                )

    def value_adapter():
        v_act = jnp.zeros(q_act.shape, jnp.float32)
        for h in range(2):
            v_act = v_act + lax.dot_general(
                v_up[h], gv_ref[h], (((1,), (1,)), ((), ())), preferred_element_type=jnp.float32
            )
            up = jnp.dot(v_down[...], gv_ref[h], preferred_element_type=jnp.float32)
            for g in range(kv_heads):
                v_bufs[0][h * kv_heads + g, :, x_ref.shape[1] // devs :] = up[
                    :, g * HEAD_SIZE : (g + 1) * HEAD_SIZE
                ].astype(jnp.bfloat16)
        project_down(v_bufs, v_act.astype(jnp.bfloat16))
        start_scatter(v_bufs)

    for d in range(1, mid):

        @pl.when(d <= ps)
        def _():
            gather_copy(small, d).wait_recv()

    for g in range(kv_heads):
        probabilities(small, g, mid, ps + 1)
    for g in range(kv_heads):
        score_gradients(small, g, mid, ps + 1)

    for d in range(1, devs):

        @pl.when(d <= ps + mid)
        def _():
            gather_copy(big, d).wait_recv()

    for g in range(kv_heads):
        probabilities(big, g, devs, ps + mid + 1)
    for g in range(kv_heads):
        score_gradients(big, g, devs, ps + mid + 1)
        if g == 0:
            collect(1, gv_ref)
            if with_adapters:
                value_adapter()

    if with_adapters:
        project_down(q_bufs, q_act[...].astype(jnp.bfloat16))
        start_scatter(q_bufs)
        start_planes(v_bufs)
        start_planes(q_bufs)
        start_spread(v_bufs)
        start_spread(q_bufs)
    collect(0, gk_ref)
    if with_adapters:
        finish(v_bufs, vd_out, vu_out, 2 * kv_heads)
        finish(q_bufs, qd_out, qu_out, devs)

    for d in range(1, devs):

        @pl.when(ps + d < devs)
        def _():
            gather_copy(small, d).wait_send()

        @pl.when(d <= ps + mid)
        def _():
            for which in range(2):
                for g in range(kv_heads):
                    return_copy(which, big, g, d).wait_send()

    for d in range(1, mid):

        @pl.when(ps + d < mid)
        def _():
            gather_copy(big, d).wait_send()

        @pl.when(d <= ps)
        def _():
            for which in range(2):
                for g in range(kv_heads):
                    return_copy(which, small, g, d).wait_send()


def attention_backward(q, do, k, v, seg, devs, adapters=None):
    tok, width = q.shape[1], q.shape[2]
    kv_heads = k.shape[2] // HEAD_SIZE
    repeat = width // k.shape[2]
    ctx = lax.axis_size("ctx")
    planes = ctx // devs
    bf16, f32 = jnp.bfloat16, jnp.float32
    vmem = pl.BlockSpec(memory_space=pltpu.VMEM)
    operands = (q, do, k, v, seg)
    results = [jax.ShapeDtypeStruct(a.shape, bf16) for a in (q, k, v)]
    scratch = [
        pltpu.VMEM((2, devs, kv_heads, tok, 2 * HEAD_SIZE), bf16),
        pltpu.VMEM((2, 2, kv_heads, devs, tok, HEAD_SIZE), bf16),
        pltpu.VMEM((2, 2, kv_heads, devs, tok, HEAD_SIZE), bf16),
        pltpu.VMEM((2, 2, kv_heads, tok, HEAD_SIZE), f32),
        pltpu.VMEM((repeat * tok, devs * tok), bf16),
        pltpu.VMEM((kv_heads, repeat * tok, devs * tok), f32),
        pltpu.VMEM((2, tok, devs * tok), f32),
        pltpu.SemaphoreType.DMA((2, devs)),
        pltpu.SemaphoreType.DMA((2, devs)),
        pltpu.SemaphoreType.DMA((2, 2, kv_heads, devs)),
        pltpu.SemaphoreType.DMA((2, 2, kv_heads, devs)),
    ]
    if adapters is not None:
        operands = operands + adapters
        x, q_down, v_down, q_up, v_up = adapters
        rank = q_down.shape[0]
        results += [jax.ShapeDtypeStruct(a.shape, f32) for a in (q_down, q_up, v_down, v_up)]
        scratch += [
            pltpu.VMEM((rank, tok), bf16),
            pltpu.VMEM((rank, tok), bf16),
            pltpu.VMEM((2, rank, q.shape[2]), bf16),
            pltpu.VMEM((2, rank, k.shape[2]), bf16),
            pltpu.VMEM((rank, tok), f32),
        ]
        for columns in ((x.shape[1] + 2 * width) // devs, x.shape[1] // devs + HEAD_SIZE):
            scratch += [
                pltpu.VMEM((n, rank, columns), bf16) for n in (devs, devs, planes, devs)
            ]
            scratch += [
                pltpu.SemaphoreType.DMA((n,)) for n in (devs, devs, planes, planes, devs, devs)
            ]
    return pl.pallas_call(
        functools.partial(attention_kernel, ctx, devs, adapters is not None),
        out_shape=tuple(results),
        in_specs=[vmem] * len(operands),
        out_specs=(vmem,) * len(results),
        scratch_shapes=scratch,
        compiler_params=pltpu.CompilerParams(
            collective_id=0, has_side_effects=True, vmem_limit_bytes=52 * 1024 * 1024
        ),
        name="attention_backward",
    )(*operands)


def on_device(
    projected_queries,
    projected_keys,
    projected_values,
    output_gradient,
    normed_layer_input,
    segment,
    query_adapter_down,
    query_adapter_up,
    value_adapter_down,
    value_adapter_up,
):
    tok_rows = projected_queries.shape[0]
    query_width = projected_queries.shape[2]
    key_width = projected_keys.shape[2]
    key_value_heads = key_width // HEAD_SIZE
    group_devs = GROUP // tok_rows
    whole_width = lax.axis_size("fsdp") == 1 and 2 * key_value_heads <= group_devs
    adapters = None
    if whole_width:
        adapters = (
            normed_layer_input,
            query_adapter_down,
            value_adapter_down,
            query_adapter_up,
            value_adapter_up,
        )
    query_grad, key_grad, value_grad, *totals = attention_backward(
        projected_queries.transpose(1, 0, 2),
        output_gradient.transpose(1, 0, 2),
        projected_keys.transpose(1, 0, 2),
        projected_values.transpose(1, 0, 2),
        segment.reshape(-1, tok_rows),
        group_devs,
        adapters,
    )
    grad_query = query_grad.transpose(1, 0, 2)
    grad_key = key_grad.transpose(1, 0, 2)
    grad_value = value_grad.transpose(1, 0, 2)
    if whole_width:
        return (grad_query, grad_key, grad_value, *totals)
    adapter_input = lax.psum(
        (
            jnp.dot(normed_layer_input, query_adapter_down.T, preferred_element_type=jnp.float32),
            jnp.dot(normed_layer_input, value_adapter_down.T, preferred_element_type=jnp.float32),
        ),
        "fsdp",
    )
    query_down_part = adapter_input[0].astype(jnp.bfloat16)
    value_down_part = adapter_input[1].astype(jnp.bfloat16)
    query_flattened_rows = grad_query.reshape(tok_rows, -1)
    value_flattened_rows = grad_value.reshape(tok_rows, -1)
    adapter_rank_rows = query_adapter_up.shape[0]
    adapter_output = lax.psum(
        (
            jnp.dot(
                query_flattened_rows,
                query_adapter_up.reshape(adapter_rank_rows, -1).T,
                preferred_element_type=jnp.float32,
            ),
            jnp.dot(
                value_flattened_rows,
                value_adapter_up.reshape(adapter_rank_rows, -1).T,
                preferred_element_type=jnp.float32,
            ),
        ),
        "fsdp",
    )
    query_up_part = adapter_output[0].astype(jnp.bfloat16)
    value_up_part = adapter_output[1].astype(jnp.bfloat16)
    local_down_query = jnp.dot(
        query_up_part.T, normed_layer_input, preferred_element_type=jnp.float32
    )
    local_up_query = jnp.dot(
        query_down_part.T, query_flattened_rows, preferred_element_type=jnp.float32
    ).reshape(adapter_rank_rows, 2, -1)
    local_down_value = jnp.dot(
        value_up_part.T, normed_layer_input, preferred_element_type=jnp.float32
    )
    local_up_value = jnp.dot(
        value_down_part.T, value_flattened_rows, preferred_element_type=jnp.float32
    ).reshape(adapter_rank_rows, 2, -1)
    gradient_totals = lax.psum(
        (local_down_query, local_up_query, local_down_value, local_up_value), "ctx"
    )
    return (
        grad_query,
        grad_key,
        grad_value,
        adapter_scale * gradient_totals[0],
        adapter_scale * gradient_totals[1],
        adapter_scale * gradient_totals[2],
        adapter_scale * gradient_totals[3],
    )


def solution(mesh):
    in_specs = (
        P(("rep", "ctx"), None, "fsdp"),
        P(("rep", "ctx"), None, "fsdp"),
        P(("rep", "ctx"), None, "fsdp"),
        P(("rep", "ctx"), None, "fsdp"),
        P(("rep", "ctx"), "fsdp"),
        P("rep"),
        P(None, "fsdp"),
        P(None, None, "fsdp"),
        P(None, "fsdp"),
        P(None, None, "fsdp"),
    )
    out_specs = (
        P(("rep", "ctx"), None, "fsdp"),
        P(("rep", "ctx"), None, "fsdp"),
        P(("rep", "ctx"), None, "fsdp"),
        P("rep", "fsdp"),
        P("rep", None, "fsdp"),
        P("rep", "fsdp"),
        P("rep", None, "fsdp"),
    )
    return jax.shard_map(
        on_device, mesh=mesh, in_specs=in_specs, out_specs=out_specs, check_vma=False
    )
```
